256 devices in a mesh: slab: 64 (over z_lo, x, y), probe: 4 (over z_hi, core).
Axes of the slice: x: 4, y: 4, z: 8 (z_hi: 2, z_lo: 4; z = z_hi * 4 + z_lo), core: 2. Of those that a mesh axis runs over, the one named last changes fastest.
Arguments:
- probes: int32 [4, 32, 1024, 512], P('probe', None, 'slab'), may hold values 0 or 1
- snapshots: float32 [4, 32, 1024, 512], P('probe', None, 'slab'), may hold values from -16 to 16
- kappa: float32 [32, 1024, 512], P(None, 'slab'), may hold values from 0.05 to 0.18
Outputs:
- precond: float32 [32, 1024, 512], P(None, 'slab', 'probe')
The draws below stay inside these ranges and needn't reach their ends.
All inputs are finite; a program needn't handle non-finite values. No bound on the sum of `probes` on one device may be relied on, other than what follows from the above.
Results may differ from the reference program's by a relative error of at most 0.00017.
Values sent between devices are 32-bit elements; how exact they have to be, the bound alone decides.
No kernel may reach another device: no remote copies, remote signals or barrier semaphores. Data moves between devices by JAX's collectives and lax.ppermute only.
A program may use at most 64 MiB of HBM per device.

```python
import math
import jax
import jax.numpy as jnp
from jax import lax

DEPTH = 32
NX = 512
NT = 4
NY = 1024
NP = 4


def draw_snapshots(key, part):
    frac_y = jnp.arange(NY, dtype=jnp.float32) / NY
    frac_x = jnp.arange(NX, dtype=jnp.float32) / NX
    scale = jnp.exp(math.log(10.0) * (0.5 * (frac_y[:, None] + frac_x[None, :]) - 0.5))
    shape = (NT, DEPTH, NY, NX)
    rough = jax.random.truncated_normal(key, -4.0, 4.0, shape, jnp.float32)
    values = scale * rough
    return values.astype(jnp.float32)


def touch_ends(array, stream_key, least, top_value):
    shape = array.shape
    spot = [jax.random.randint(jax.random.fold_in(stream_key, axis), (), 0, shape[axis]) for axis in range(len(shape))]
    array = array.at[tuple(spot)].set(least)
    longest = shape.index(max(shape))
    spot[longest] = (spot[longest] + 1) % shape[longest]
    return array.at[tuple(spot)].set(top_value)


def levels(rng, dims, split, low, high):
    loudness, own = 1.0, jax.random.fold_in(rng, 6)
    for axis_at, parts in split:
        heights = jnp.exp(jax.random.uniform(jax.random.fold_in(own, axis_at), (parts,), jnp.float32, low / len(split), high / len(split)))
        loudness = loudness * jnp.repeat(heights, dims[axis_at] // parts).reshape([-1 if axis == axis_at else 1 for axis in range(len(dims))])
    return loudness


def setup_inputs(seed: int = 0) -> dict:
    key_list = jax.random.split(jax.random.key(seed), 4)
    probes = touch_ends((jax.random.randint(key_list[0], (NP, DEPTH, NY, NX), 0, 2) < 1).astype(jnp.int32), jax.random.fold_in(key_list[0], 1), 0, 1)
    snapshots = draw_snapshots(jax.random.fold_in(key_list[3], 71), 0)
    kappa = jnp.clip(jnp.exp(math.log(0.18) - 1.2809339 * jax.random.uniform(key_list[2], (DEPTH, NY, NX), jnp.float32) ** levels(key_list[2], (DEPTH, NY, NX), ((1, 64),), -0.2, 0.2)), 0.05, 0.18)
    return dict(probes=probes, snapshots=snapshots, kappa=kappa)


COEFFS = (-205.0 / 72.0, 8.0 / 5.0, -1.0 / 5.0, 8.0 / 315.0, -1.0 / 560.0)
EPSILON = 1e-06

def stencil(padded, n_depth, n_rows, n_width):
    centre = padded[:, 4:4 + n_depth, 4:4 + n_rows, 4:4 + n_width]
    summed = 3.0 * COEFFS[0] * centre
    for offset in range(1, 5):
        paired = padded[:, 4 + offset:4 + offset + n_depth, 4:4 + n_rows, 4:4 + n_width]
        paired = paired + padded[:, 4 - offset:4 - offset + n_depth, 4:4 + n_rows, 4:4 + n_width]
        paired = paired + padded[:, 4:4 + n_depth, 4 + offset:4 + offset + n_rows, 4:4 + n_width]
        paired = paired + padded[:, 4:4 + n_depth, 4 - offset:4 - offset + n_rows, 4:4 + n_width]
        paired = paired + padded[:, 4:4 + n_depth, 4:4 + n_rows, 4 + offset:4 + offset + n_width]
        paired = paired + padded[:, 4:4 + n_depth, 4:4 + n_rows, 4 - offset:4 - offset + n_width]
        summed = summed + COEFFS[offset] * paired
    return summed

def laplace(field):
    padded = jnp.pad(field, ((0, 0), (4, 4), (4, 4), (4, 4)))
    return stencil(padded, field.shape[1], field.shape[2], field.shape[3])

def reference(probes, snapshots, kappa):
    coeff_field = kappa[None]

    def one_probe(carry, mask):
        signs = (2 * mask - 1).astype(jnp.float32)[None]
        previous = jnp.zeros_like(signs)
        current = signs * snapshots[0][None]
        scattered = [current]
        for moment in range(1, NT):
            following = 2.0 * current - previous + coeff_field * laplace(current) + signs * snapshots[moment][None]
            previous = current
            current = following
            scattered.append(current)
        later = jnp.zeros_like(signs)
        adjoint = scattered[NT - 1]
        image = snapshots[NT - 1][None] * adjoint
        for moment in range(NT - 2, -1, -1):
            earlier = scattered[moment] + 2.0 * adjoint - later + laplace(coeff_field * adjoint)
            later = adjoint
            adjoint = earlier
            image = image + snapshots[moment][None] * adjoint
        return (carry + (signs * image)[0], None)
    start = jnp.zeros(kappa.shape, jnp.float32)
    estimate, unused = lax.scan(one_probe, start, probes)
    return estimate / jnp.sqrt(jnp.mean(estimate * estimate) + EPSILON)
```

```python
import functools

import jax
import jax.numpy as jnp
from jax import lax
from jax.experimental import pallas as pl
from jax.experimental.pallas import tpu as pltpu
from jax.sharding import PartitionSpec as P

NT = 4
COEFFS = (-205.0 / 72.0, 8.0 / 5.0, -1.0 / 5.0, 8.0 / 315.0, -1.0 / 560.0)
EPSILON = 1e-06
AXES = ("slab", "probe")
ROW = (16, 8, 128)
HALF = (4,) + ROW
VLIM = 12 * 1024 * 1024


def call(body, outs, n_smem, n_vmem, flops=1 << 20, nbytes=1 << 20, name=None):
    return pl.pallas_call(
        body,
        out_shape=[jax.ShapeDtypeStruct(s, jnp.float32) for s in outs],
        in_specs=[pl.BlockSpec(memory_space=pltpu.SMEM)] * n_smem
        + [pl.BlockSpec(memory_space=pltpu.VMEM)] * n_vmem,
        out_specs=[pl.BlockSpec(memory_space=pltpu.VMEM) for _ in outs],
        compiler_params=pltpu.CompilerParams(vmem_limit_bytes=VLIM),
        cost_estimate=pl.CostEstimate(flops=flops, bytes_accessed=nbytes, transcendentals=0),
        name=name,
    )


def place(y):
    owner = y // 8
    j = y if owner == 0 else 15 - y
    half = j // 4
    return owner, half, (j if half == 0 else 7 - j)


def pick(rows_ref, y, zl, zh):
    start = ((zh * 16 + zl) * 2 + y // 8) * 32 + y % 8
    return rows_ref[pl.ds(start, 4, stride=8), :]


def pack_u(flags, rows_ref, out_ref):
    core = flags[0]

    def step(zl, carry):
        for y in range(16):
            owner, half, k = place(y)
            slot = jnp.where(core == owner, 0, 1)
            for zh in range(2):
                out_ref[slot, half, k, zl, zh * 4 : zh * 4 + 4, :] = pick(rows_ref, y, zl, zh)
        return carry

    lax.fori_loop(0, 16, step, 0)


def pack_sk(flags, probe_ref, kappa_ref, sign_ref, k_ref):
    core = flags[0]

    def step(zl, carry):
        for y in range(16):
            owner, half, k = place(y)
            slot = jnp.where(core == owner, 0, 1)
            for zh in range(2):
                bits = pick(probe_ref, y, zl, zh)
                sign_ref[slot, half, k, zl, zh * 4 : zh * 4 + 4, :] = (2 * bits - 1).astype(jnp.float32)
                k_ref[slot, half, k, zl, zh * 4 : zh * 4 + 4, :] = pick(kappa_ref, y, zl, zh)
        return carry

    lax.fori_loop(0, 16, step, 0)


def sort_u(flags, own_ref, got_ref, even_ref, oddo_ref, oddi_ref):
    first = flags[0] == 0

    def step(k, carry):
        for half in range(2):
            own, got = own_ref[0, half, k], got_ref[half, k]
            even_ref[half, k] = jnp.where(first, own, got)
            (oddo_ref if half == 0 else oddi_ref)[k] = jnp.where(first, got, own)
        return carry

    lax.fori_loop(0, 4, step, 0)


def sort_s(flags, own_ref, got_ref, so_ref, si_ref):
    first = flags[0] == 0

    def step(k, carry):
        for half in range(2):
            own, got = own_ref[0, half, k], got_ref[half, k]
            out = so_ref if half == 0 else si_ref
            out[0, k] = jnp.where(first, own, got)
            out[1, k] = jnp.where(first, got, own)
        return carry

    lax.fori_loop(0, 4, step, 0)


def start_fields(flags, le_ref, re_ref, so_ref, si_ref, fo_ref, fi_ref):
    low = flags[1] == 0

    def step(k, carry):
        for half in range(2):
            u = jnp.where(low, le_ref[half, k], re_ref[half, k])
            s_ref, f_ref = (so_ref, fo_ref) if half == 0 else (si_ref, fi_ref)
            for p in range(2):
                f_ref[p, k] = s_ref[p, k] * u
        return carry

    lax.fori_loop(0, 4, step, 0)


def laplace_row(rows, k):
    centre = rows[k + 4]
    sub = lax.broadcasted_iota(jnp.int32, (1, 8, 128), 1)
    lane = lax.broadcasted_iota(jnp.int32, (1, 8, 128), 2)
    upper = sub >= 4
    tile = sub % 4
    zero = jnp.zeros((1, 8, 128), jnp.float32)
    above = jnp.where(upper, pltpu.roll(centre[12:16], 4, 1), zero)
    below = jnp.where(upper, zero, pltpu.roll(centre[0:4], 4, 1))
    column = jnp.concatenate([above, centre, below], axis=0)
    following = jnp.where(tile == 3, zero, pltpu.roll(centre, 7, 1))
    preceding = jnp.where(tile == 0, zero, pltpu.roll(centre, 1, 1))
    edge = jnp.where(lane < 64, following, preceding)
    total = (3.0 * COEFFS[0]) * centre
    for j in range(1, 5):
        paired = column[4 + j : 20 + j] + column[4 - j : 20 - j]
        paired = paired + (rows[k + 4 + j] + rows[k + 4 - j])
        paired = paired + pltpu.roll(jnp.where(lane >= j, centre, edge), 128 - j, 2)
        paired = paired + pltpu.roll(jnp.where(lane < 128 - j, centre, edge), j, 2)
        total = total + COEFFS[j] * paired
    return total


def rows_of(open_, halo_ref, near_ref, far_ref, p):
    halo = [jnp.where(open_, halo_ref[p, 3 - i], 0.0) for i in range(4)]
    return halo + [near_ref[p, i] for i in range(4)] + [far_ref[p, 3 - i] for i in range(4)]


def forward(outer, first, last, flags, *refs):
    refs = list(refs)
    halo_ref, near_ref, far_ref, s_ref, k_ref, lu_ref, ru_ref = refs[:7]
    old_ref = None if first else refs[7]
    outs = refs[7:] if first else refs[8:]
    low = flags[1] == 0 if not last[1] else flags[1] != 0
    open_ = flags[2] == 0 if outer else True

    def step(p, carry):
        rows = rows_of(open_, halo_ref, near_ref, far_ref, p)
        for k in range(4):
            u = jnp.where(low, lu_ref[k], ru_ref[k])
            value = 2.0 * rows[k + 4] + k_ref[k] * laplace_row(rows, k) + s_ref[p, k] * u
            if not first:
                value = value - old_ref[p, k]
            outs[0][p, k] = value
            if last[0]:
                outs[1][p, k] = k_ref[k] * value
        return carry

    lax.fori_loop(0, 2, step, 0)


def backward(outer, first, flags, *refs):
    refs = list(refs)
    halo_ref, near_ref, far_ref, f_ref, a_ref, k_ref = refs[:6]
    later_ref = None if first else refs[6]
    a_out, g_out = refs[-2:]
    open_ = flags[2] == 0 if outer else True

    def step(p, carry):
        rows = rows_of(open_, halo_ref, near_ref, far_ref, p)
        for k in range(4):
            value = f_ref[p, k] + 2.0 * a_ref[p, k] + laplace_row(rows, k)
            if not first:
                value = value - later_ref[p, k]
            a_out[p, k] = value
            g_out[p, k] = k_ref[k] * value
        return carry

    lax.fori_loop(0, 2, step, 0)


def finish(outer, flags, *refs):
    (halo_ref, near_ref, far_ref, f1_ref, f4_ref, a3_ref, a2_ref, s_ref) = refs[:8]
    le_ref, re_ref, lo_ref, ro_ref, est_ref = refs[8:]
    low = flags[1] == 0
    open_ = flags[2] == 0 if outer else True

    def step(p, carry):
        rows = rows_of(open_, halo_ref, near_ref, far_ref, p)
        for k in range(4):
            a1 = f1_ref[p, k] + 2.0 * a2_ref[p, k] - a3_ref[p, k] + laplace_row(rows, k)
            u0, u2 = jnp.where(low, le_ref[k], re_ref[k]), jnp.where(low, re_ref[k], le_ref[k])
            u1, u3 = jnp.where(low, lo_ref[k], ro_ref[k]), jnp.where(low, ro_ref[k], lo_ref[k])
            image = u3 * f4_ref[p, k] + u2 * a3_ref[p, k] + u1 * a2_ref[p, k] + u0 * a1
            est_ref[k] = jnp.where(p == 0, 0.0, est_ref[k]) + s_ref[p, k] * image
        return carry

    lax.fori_loop(0, 2, step, 0)


def spread(flags, eo_ref, ei_ref, keep_ref, give_ref):
    low = flags[1] == 0
    for half, ref in ((0, eo_ref), (1, ei_ref)):
        for k in range(4):
            j = k if half == 0 else 7 - k

            def step(zl, carry, ref=ref, k=k, j=j):
                value = ref[k, zl]
                for zh in range(2):
                    row = j * 32 + zh * 16 + zl
                    lo, hi = value[zh * 4 : zh * 4 + 2], value[zh * 4 + 2 : zh * 4 + 4]
                    keep_ref[pl.ds(row, 2, stride=256), :] = jnp.where(low, lo, hi)
                    give_ref[pl.ds(row, 2, stride=256), :] = jnp.where(low, hi, lo)
                return carry

            lax.fori_loop(0, 16, step, 0)


def reduce_body(flags, keep_ref, got_ref, mine_ref, give_ref, sq_ref):
    first = flags[0] == 0
    total = jnp.zeros((8, 128), jnp.float32)
    for i in range(8):
        lo = keep_ref[pl.ds(i * 32, 32), :] + got_ref[pl.ds(i * 32, 32), :]
        hi = keep_ref[pl.ds(256 + i * 32, 32), :] + got_ref[pl.ds(256 + i * 32, 32), :]
        mine_ref[pl.ds(i * 32, 32), :] = jnp.where(first, lo, hi)
        give_ref[pl.ds(i * 32, 32), :] = jnp.where(first, hi, lo)
        total = total + jnp.sum((lo * lo + hi * hi).reshape(4, 8, 128), axis=0)
    part = jnp.sum(jnp.sum(total, axis=0, keepdims=True), axis=1, keepdims=True)
    sq_ref[...] = jnp.broadcast_to(part, sq_ref.shape)


def scale_body(cells, flags, sq_ref, mine_ref, got_ref, out_ref):
    squares = jnp.sum(sq_ref[...], axis=0, keepdims=True)
    factor = lax.rsqrt(squares / cells + EPSILON)
    for core in range(2):

        @pl.when(flags[0] == core)
        def _():
            for j in range(8):
                rows = (j, 15 - j) if core == 0 else (15 - j, j)
                out_ref[pl.ds(rows[0], 32, stride=16), :] = mine_ref[pl.ds(j * 32, 32), :] * factor
                out_ref[pl.ds(rows[1], 32, stride=16), :] = got_ref[pl.ds(j * 32, 32), :] * factor


def rows_view(x):
    return x.reshape(32, 2, 8, 4, 128).transpose(0, 1, 3, 2, 4).reshape(2048, 128)


def body(probes, snapshots, kappa):
    n_slab, n_probe = lax.axis_size("slab"), lax.axis_size("probe")
    n = n_slab * n_probe
    slab, probe = lax.axis_index("slab"), lax.axis_index("probe")
    core, chip = probe % 2, probe // 2
    ends = ((core == 0) & (slab == 0)) | ((core == 1) & (slab == n_slab - 1))
    flags = jnp.stack([core, chip, ends.astype(jnp.int32)]).astype(jnp.int32)

    def across(x):
        return lax.ppermute(x, AXES, [(i, i ^ 1) for i in range(n)])

    def over(x):
        return lax.ppermute(x, AXES, [(i, i ^ 2) for i in range(n)])

    pairs = []
    for i in range(n):
        s, p = divmod(i, n_probe)
        hi, c = divmod(p, 2)
        t = s + 1 if c == 1 else s - 1
        if t in (-1, n_slab):
            t, hi = t % n_slab, 1 - hi
        pairs.append((i, t * n_probe + hi * 2 + 1 - c))

    def along(x):
        return lax.ppermute(x, AXES, pairs)

    both = (2,) + HALF
    packed = (2, 2) + HALF
    (u_pack,) = call(pack_u, [packed], 1, 1, name="pack_u")(flags, rows_view(snapshots))
    u_got = across(u_pack[1])
    s_pack, k_pack = call(pack_sk, [packed, packed], 1, 2, name="pack_sk")(
        flags, rows_view(probes), rows_view(kappa)
    )
    s_got = across(s_pack[1])
    even, odd_o, odd_i = call(sort_u, [both, HALF, HALF], 1, 2, name="sort_u")(flags, u_pack, u_got)
    r_even = over(even)
    r_odd_o = over(odd_o)
    r_odd_i = over(odd_i)
    signs = call(sort_s, [both, both], 1, 2, name="sort_s")(flags, s_pack, s_got)
    kap = (k_pack[0, 0], k_pack[0, 1])
    ev, rev = (even[0], even[1]), (r_even[0], r_even[1])
    odd, rodd = (odd_o, odd_i), (r_odd_o, r_odd_i)

    f1 = call(start_fields, [both, both], 1, 4, name="start")(flags, even, r_even, *signs)

    def halos(f):
        return along(f[0]), across(f[1])

    def halves(make):
        inner = make(1)
        outer = make(0)
        return outer, inner

    def fwd(f, old, u, ru, last, name):
        halo = halos(f)

        def make(h):
            ins = [halo[h], f[h], f[1 - h], signs[h], kap[h], u[h], ru[h]]
            if old is not None:
                ins.append(old[h])
            outs = [both] * (2 if last[0] else 1)
            kern = functools.partial(forward, h == 0, old is None, last)
            return call(kern, outs, 1, len(ins), name=name + "oi"[h])(flags, *ins)

        outer, inner = halves(make)
        return [(outer[i], inner[i]) for i in range(len(outer))]

    (f2,) = fwd(f1, None, odd, rodd, (False, False), "f2")
    (f3,) = fwd(f2, f1, ev, rev, (False, True), "f3")
    f4, g4 = fwd(f3, f2, odd, rodd, (True, True), "f4")

    def bwd(g, f, a, later, name):
        halo = halos(g)

        def make(h):
            ins = [halo[h], g[h], g[1 - h], f[h], a[h], kap[h]]
            if later is not None:
                ins.append(later[h])
            kern = functools.partial(backward, h == 0, later is None)
            return call(kern, [both, both], 1, len(ins), name=name + "oi"[h])(flags, *ins)

        outer, inner = halves(make)
        return [(outer[i], inner[i]) for i in range(2)]

    a3, g3 = bwd(g4, f3, f4, None, "a3")
    a2, g2 = bwd(g3, f2, a3, f4, "a2")
    halo = halos(g2)

    def last(h):
        ins = [halo[h], g2[h], g2[1 - h], f1[h], f4[h], a3[h], a2[h], signs[h]]
        ins += [ev[h], rev[h], odd[h], rodd[h]]
        kern = functools.partial(finish, h == 0)
        return call(kern, [HALF], 1, len(ins), name="a1" + "oi"[h])(flags, *ins)[0]

    est_i = last(1)
    est_o = last(0)
    keep, give = call(spread, [(512, 128), (512, 128)], 1, 2, name="spread")(flags, est_o, est_i)
    got = over(give)
    mine, send, squares = call(
        reduce_body, [(256, 128), (256, 128), (n, 128)], 1, 2, name="reduce"
    )(flags, keep, got)
    theirs = across(send)
    squares = lax.all_to_all(squares, AXES, 0, 0, tiled=True)
    cells = 32.0 * 16.0 * 512.0 * n_slab
    (out,) = call(functools.partial(scale_body, cells), [(512, 128)], 1, 3, name="scale")(
        flags, squares, mine, theirs
    )
    return out.reshape(32, 16, 128)


def solution(mesh):
    return jax.shard_map(
        body,
        mesh=mesh,
        in_specs=(
            P("probe", None, "slab", None),
            P("probe", None, "slab", None),
            P(None, "slab", None),
        ),
        out_specs=P(None, "slab", "probe"),
        check_vma=False,
    )
```
